32 devices in a mesh: dp: 8 (over y, x, core), ctx: 4 (over z).
Axes of the slice: x: 2, y: 2, z: 4, core: 2. Of those that a mesh axis runs over, the one named last changes fastest.
Arguments:
- tokens: bfloat16 [1024, 8, 1024], P('ctx', 'dp'), may hold values from -6 to 6
- cotangent: bfloat16 [1024, 8, 1024], P('ctx', 'dp'), may hold values from -6 to 6
- segments: int32 [8, 1024], P('dp'), may hold values from 0 to 1, never falling along the last dimension, each value on 1 to 768 neighbouring positions
- qkv_weight: float32 [1024, 3072], P(None, ('dp', 'ctx')), may hold values from -2 to 2
- output_weight: float32 [1024, 1024], P(None, ('dp', 'ctx')), may hold values from -0.375 to 0.375
- hidden_weight: float32 [1024, 4096], P(None, ('dp', 'ctx')), may hold values from -0.1875 to 0.1875
- down_weight: float32 [4096, 1024], P(('dp', 'ctx')), may hold values from -0.09375 to 0.09375
- small_params: float32 [12288], P(('dp', 'ctx')), may hold values from -2.5 to 2.5
- qkv_moment: float32 [1024, 3072], P(None, ('dp', 'ctx')), may hold values from -27.1529 to 27.1529
- output_moment: float32 [1024, 1024], P(None, ('dp', 'ctx')), may hold values from -27.1529 to 27.1529
- hidden_moment: float32 [1024, 4096], P(None, ('dp', 'ctx')), may hold values from -27.1529 to 27.1529
- down_moment: float32 [4096, 1024], P(('dp', 'ctx')), may hold values from -27.1529 to 27.1529
- adam_first: float32 [12288], P(('dp', 'ctx')), may hold values from -10 to 10
- adam_second: float32 [12288], P(('dp', 'ctx')), may hold values from 8.192 to 163.84
Outputs:
- block_out: bfloat16 [1024, 8, 1024], P('ctx', 'dp')
- input_grad: float32 [1024, 8, 1024], P('ctx', 'dp')
- qkv_grad: float32 [1024, 3072], P(None, ('dp', 'ctx'))
- output_grad: float32 [1024, 1024], P(None, ('dp', 'ctx'))
- hidden_grad: float32 [1024, 4096], P(None, ('dp', 'ctx'))
- down_grad: float32 [4096, 1024], P(('dp', 'ctx'))
- small_grad: float32 [12288], P(('dp', 'ctx'))
- new_qkv: float32 [1024, 3072], P(None, ('dp', 'ctx'))
- new_output: float32 [1024, 1024], P(None, ('dp', 'ctx'))
- new_hidden: float32 [1024, 4096], P(None, ('dp', 'ctx'))
- new_down: float32 [4096, 1024], P(('dp', 'ctx'))
- new_small: float32 [12288], P(('dp', 'ctx'))
- new_qkv_moment: float32 [1024, 3072], P(None, ('dp', 'ctx'))
- new_output_moment: float32 [1024, 1024], P(None, ('dp', 'ctx'))
- new_hidden_moment: float32 [1024, 4096], P(None, ('dp', 'ctx'))
- new_down_moment: float32 [4096, 1024], P(('dp', 'ctx'))
- new_first: float32 [12288], P(('dp', 'ctx'))
- new_second: float32 [12288], P(('dp', 'ctx'))
The draws below stay inside these ranges and needn't reach their ends.
Inputs may be any that keep to these rules, and one draw needn't show every extreme that they name: `segments`: segment numbers never fall along a sequence; each document spans 1 to 768 positions.
All inputs are finite; a program needn't handle non-finite values.
Results may differ from the reference program's by a relative error of at most 0.025.
Values may be sent and summed in bfloat16 or wider, within the bound.
No kernel may reach another device: no remote copies, remote signals or barrier semaphores. Data moves between devices by JAX's collectives and lax.ppermute only.
A program may use at most 192 MiB of HBM per device.

```python
import math
import jax
import jax.numpy as jnp
import numpy as np
from jax import lax

D = 1024
H = 16
HD = 64
FF = 4096
LEN = 1024
ITERS = 5
STEP = 4
SEQS = 8


def draw_qkv_weight(key, part):
    first = jax.random.fold_in(jax.random.fold_in(key, 17), 0)
    return jax.random.normal(first, (D, 3 * D), jnp.float32) / math.sqrt(D)


def draw_small_params(key, part):
    first, second, third = jax.random.split(jax.random.fold_in(key, 29), 3)
    biases = jnp.clip(jax.random.normal(first, (4 * D + FF,), jnp.float32), -8.0, 8.0) * 0.2
    spread = jax.random.uniform(second, (4 * D,), jnp.float32, -0.4, 0.4)
    shifts = jnp.clip(jax.random.normal(third, (4 * D,), jnp.float32), -8.0, 8.0) * 0.2
    which = jnp.arange(4 * D, dtype=jnp.int32) // D
    norm_part = jnp.where(which % 2 == 0, jnp.exp(spread), shifts)
    return jnp.concatenate([biases, norm_part])


def moment_like(key, salt, height, breadth):
    first, second, third, fourth = jax.random.split(jax.random.fold_in(key, salt), 4)
    scale = 0.05 * math.sqrt(SEQS * LEN)
    shorter = min(height, breadth)
    inner_rank = min(100, shorter // 2)
    left = jax.random.normal(first, (height, inner_rank), jnp.float32)
    right = jax.random.normal(second, (breadth, inner_rank), jnp.float32)
    spectrum = jax.random.uniform(third, (inner_rank,), jnp.float32, 0.8, 1.2)
    noise = jax.random.normal(fourth, (height, breadth), jnp.float32)
    weighted = left * (spectrum / math.sqrt(inner_rank))[None, :]
    flat = jnp.dot(weighted, right.T, precision=lax.Precision.HIGHEST, preferred_element_type=jnp.float32)
    return jnp.clip((flat + 0.1 * noise) * scale, -6.0 * scale, 6.0 * scale)


def draw_qkv_moment(key, part):
    return moment_like(key, 41, D, 3 * D)


def draw_output_moment(key, part):
    return moment_like(key, 43, D, D)


def draw_hidden_moment(key, part):
    return moment_like(key, 47, D, FF)


def draw_down_moment(key, part):
    return moment_like(key, 53, FF, D)


def shard_levels(own_key, extent, shards, least, largest):
    def one(dim, parts):
        draws = jax.random.uniform(jax.random.fold_in(jax.random.fold_in(own_key, 6), dim), (parts,), jnp.float32, least / len(shards), largest / len(shards))
        return jnp.repeat(jnp.exp(draws), extent[dim] // parts).reshape((-1,) + (1,) * (len(extent) - dim - 1))

    level = one(*shards[0])
    for cut in shards[1:]:
        level = level * one(*cut)
    return level


def profile(amount, total, reach, slope):
    weights = [(1 << 20) // math.isqrt(rank ** slope) + 1 for rank in range(2, amount + 1)]
    spare, counts = total - reach - (amount - 1), [1] * (amount - 1)
    while spare > 0:
        movable = [i for i in range(amount - 1) if counts[i] < reach]
        mass, left = sum([weights[i] for i in movable]), spare
        for i in movable:
            addition = min(reach - counts[i], max(1, left * weights[i] // mass), spare)
            counts[i] = counts[i] + addition
            spare = spare - addition
    return np.array([reach] + counts)


def uneven_parts(stream_key, count, total, bound, skew):
    if count == 2:
        one = jax.random.randint(stream_key, (), max(1, total - bound), min(bound, total - 1) + 1)
        return jnp.stack([one, total - one])
    lengths = jnp.asarray(profile(count, total, bound, skew), jnp.int32)
    twos = (count - 1) // 2
    source_of, taker = lengths[1:1 + 2 * twos:2], lengths[2:2 + 2 * twos:2]
    room = jnp.minimum(source_of - 1, bound - taker)
    shifted = jax.random.randint(jax.random.fold_in(stream_key, 1), (twos,), 0, 1 << 20) % (room + 1)
    lengths = lengths.at[1:1 + 2 * twos:2].set(source_of - shifted).at[2:2 + 2 * twos:2].set(taker + shifted)
    return lengths[jax.random.permutation(jax.random.fold_in(stream_key, 2), count)]


def scatter_about(key, extent, scale, bound, cuts=(), kind=jnp.bfloat16):
    array = scale * jax.random.normal(key, extent, jnp.float32)
    if cuts:
        array = array * shard_levels(key, extent, cuts, -0.22, 0.18)
    return jnp.clip(array, -bound, bound).astype(kind)


def setup_inputs(seed: int = 0) -> dict:
    splits = jax.random.split(jax.random.key(seed), 15)
    return {
        "tokens": scatter_about(splits[0], (LEN, SEQS, D), 1.0, 6.0, ((0, 4), (1, 8))),
        "cotangent": scatter_about(splits[1], (LEN, SEQS, D), 1.0, 6.0, ((0, 4), (1, 8))),
        "segments": jax.vmap(lambda own: jnp.searchsorted(jnp.cumsum(uneven_parts(own, 2, LEN, 3 * LEN // 4, 0)), jnp.arange(LEN), side="right"))(jax.random.split(splits[2], SEQS)).reshape((SEQS, LEN)).astype(jnp.int32),
        "qkv_weight": draw_qkv_weight(jax.random.fold_in(splits[14], 71), 0),
        "output_weight": scatter_about(splits[4], (D, D), (D // 4) ** -0.5, 0.375, ((1, 32),), jnp.float32),
        "hidden_weight": scatter_about(splits[5], (D, FF), D ** -0.5, 0.1875, ((1, 32),), jnp.float32),
        "down_weight": scatter_about(splits[6], (FF, D), FF ** -0.5, 0.09375, ((0, 32),), jnp.float32),
        "small_params": draw_small_params(jax.random.fold_in(splits[14], 71), 0),
        "qkv_moment": draw_qkv_moment(jax.random.fold_in(splits[14], 71), 0),
        "output_moment": draw_output_moment(jax.random.fold_in(splits[14], 71), 0),
        "hidden_moment": draw_hidden_moment(jax.random.fold_in(splits[14], 71), 0),
        "down_moment": draw_down_moment(jax.random.fold_in(splits[14], 71), 0),
        "adam_first": scatter_about(splits[12], (8 * D + FF,), (0.02 * (SEQS * LEN) ** 0.5), 10.0, ((0, 32),), jnp.float32),
        "adam_second": jnp.clip(jnp.exp(math.log(163.84) - 2.9957322 * jax.random.uniform(splits[13], (8 * D + FF,), jnp.float32) ** shard_levels(splits[13], (8 * D + FF,), ((0, 32),), -0.2, 0.2)), 8.192, 163.84),
    }


poly_linear = 3.4445
poly_cubic = -4.775
poly_quintic = 2.0315
momentum_rate = 0.95
muon_rate = 0.05
muon_step = 0.05
decay_rate = 0.1
adam_rate = 0.5
beta_first = 0.9
beta_second = 0.95

@jax.custom_vjp
def low(v):
    return lax.optimization_barrier(v.astype(jnp.bfloat16)).astype(jnp.float32)

@jax.custom_vjp
def low_back(v):
    return v

def low_keep(v):
    return (low(v), None)

def low_pass(kept, grad):
    return (grad,)

def back_keep(v):
    return (v, None)

def back_low(kept, grad):
    return (low(grad),)
low.defvjp(low_keep, low_pass)
low_back.defvjp(back_keep, back_low)

def matmul(left, right):
    return jnp.dot(left, right, precision=lax.Precision.HIGHEST, preferred_element_type=jnp.float32)

def norm_rows(values, gain, shift):
    center = values - lax.optimization_barrier(jnp.mean(values, axis=-1, keepdims=True))
    spread = lax.optimization_barrier(jnp.mean(center * center, axis=-1, keepdims=True))
    return center * lax.rsqrt(spread + 1e-05) * gain + shift

def split_small(packed):
    pieces = []
    offset = 0
    for width in (D, D, D, FF, D, D, D, D, D):
        pieces.append(packed[offset:offset + width])
        offset = offset + width
    return pieces

def forward(params, inputs, seg_ids):
    qkv_w = low(params[0])
    output_w = low(params[1])
    hidden_w = low(params[2])
    down_w = low(params[3])
    query_bias, value_bias, output_bias, hidden_bias, down_bias, attn_gain, attn_shift, mlp_gain, mlp_shift = split_small(low(params[4]))
    group = inputs.shape[0]
    length = inputs.shape[1]
    rows = inputs.reshape(group * length, D)
    normed_one = low(norm_rows(rows, attn_gain, attn_shift))
    bias = jnp.concatenate([query_bias, jnp.zeros((D,), jnp.float32), value_bias])
    qkv = low(low_back(matmul(normed_one, qkv_w) + bias))
    query = qkv[:, :D].reshape(group, length, H, HD)
    keys = qkv[:, D:2 * D].reshape(group, length, H, HD)
    values = qkv[:, 2 * D:].reshape(group, length, H, HD)
    rows_block = min(512, length)
    blocks = length // rows_block
    positions = jnp.arange(length, dtype=jnp.int32)

    def attend(index):
        start = index * rows_block
        query_block = lax.dynamic_slice_in_dim(query, start, rows_block, 1)
        scores = jnp.einsum('gqhd,gkhd->ghqk', query_block, keys, precision=lax.Precision.HIGHEST) * 0.125
        scores = low_back(scores)
        query_pos = start + jnp.arange(rows_block, dtype=jnp.int32)
        seg_query = lax.dynamic_slice_in_dim(seg_ids, start, rows_block, 1)
        allowed = (positions[None, None, :] <= query_pos[None, :, None]) & (seg_query[:, :, None] == seg_ids[:, None, :])
        scores = jnp.where(allowed[:, None], scores, -1e+30)
        weights = low(jax.nn.softmax(scores, axis=-1))
        return jnp.einsum('ghqk,gkhd->gqhd', weights, values, precision=lax.Precision.HIGHEST)
    mixed = lax.map(jax.checkpoint(attend), jnp.arange(blocks, dtype=jnp.int32))
    mixed = jnp.transpose(mixed, (1, 0, 2, 3, 4)).reshape(group * length, D)
    mix_low = low(low_back(mixed))
    middle = rows + low_back(matmul(mix_low, output_w) + output_bias)
    normed_two = low(norm_rows(middle, mlp_gain, mlp_shift))
    hidden_pre = low_back(matmul(normed_two, hidden_w) + hidden_bias)
    act = low(jax.nn.gelu(hidden_pre, approximate=True))
    result = middle + matmul(act, down_w) + down_bias
    return result.reshape(group, length, D)

def newton(matrix, tall):

    def gram_of(value):
        if tall:
            return matmul(value.T, value)
        return matmul(value, value.T)
    gram = gram_of(matrix)
    scale = jnp.sqrt(jnp.trace(gram)) + 1e-07
    matrix = matrix / scale
    gram = gram / (scale * scale)
    for sweep in range(ITERS):
        if tall:
            once = matmul(matrix, gram)
            twice = matmul(once, gram)
        else:
            once = matmul(gram, matrix)
            twice = matmul(gram, once)
        matrix = poly_linear * matrix + poly_cubic * once + poly_quintic * twice
        if sweep + 1 < ITERS:
            gram = gram_of(matrix)
    return matrix

def reference(tokens, cotangent, segments, qkv_weight, output_weight, hidden_weight, down_weight, small_params, qkv_moment, output_moment, hidden_moment, down_moment, adam_first, adam_second):
    params = (qkv_weight, output_weight, hidden_weight, down_weight, small_params)
    group = math.gcd(SEQS, max(1, 4096 // LEN))
    count = SEQS // group
    inputs = jnp.transpose(tokens.astype(jnp.float32), (1, 0, 2)).reshape(count, group, LEN, D)
    pulls = jnp.transpose(cotangent.astype(jnp.float32), (1, 0, 2)).reshape(count, group, LEN, D)
    seg_groups = segments.reshape(count, group, LEN)

    def advance(total, items):
        block_in, block_pull, block_seg = items
        outputs, pull = jax.vjp(lambda p, v: forward(p, v, block_seg), params, block_in)
        grads, grad_in = pull(block_pull)
        return (jax.tree.map(jnp.add, total, grads), (outputs, grad_in))
    zeros = jax.tree.map(jnp.zeros_like, params)
    grads, (outputs, grad_inputs) = lax.scan(advance, zeros, (inputs, pulls, seg_groups))
    block_out = jnp.transpose(outputs.reshape(SEQS, LEN, D), (1, 0, 2)).astype(jnp.bfloat16)
    input_grad = jnp.transpose(grad_inputs.reshape(SEQS, LEN, D), (1, 0, 2))
    moments = (qkv_moment, output_moment, hidden_moment, down_moment)
    tall_flags = (False, False, False, True)
    new_moments = []
    new_weights = []
    for index in range(4):
        moment = momentum_rate * moments[index] + grads[index]
        new_moments.append(moment)
        ortho = newton(moment, tall_flags[index])
        weight = params[index]
        factor = muon_step * math.sqrt(max(weight.shape[0], weight.shape[1]))
        new_weights.append(weight * (1.0 - muon_rate * decay_rate) - factor * ortho)
    small_g = grads[4]
    new_first = beta_first * adam_first + (1.0 - beta_first) * small_g
    new_second = beta_second * adam_second + (1.0 - beta_second) * small_g * small_g
    corrected = new_first / (1.0 - beta_first ** STEP) / (jnp.sqrt(new_second / (1.0 - beta_second ** STEP)) + 1e-08)
    new_small = small_params - adam_rate * corrected
    return (block_out, input_grad, grads[0], grads[1], grads[2], grads[3], grads[4], new_weights[0], new_weights[1], new_weights[2], new_weights[3], new_small, new_moments[0], new_moments[1], new_moments[2], new_moments[3], new_first, new_second)
```

```python
import math

import jax
import jax.numpy as jnp
from jax import lax
from jax.experimental import pallas as pl
from jax.experimental.pallas import tpu as pltpu
from jax.sharding import PartitionSpec as P

D = 1024
H = 16
HD = 64
FF = 4096
ITERS = 5
STEP = 4

poly_linear = 3.4445
poly_cubic = -4.775
poly_quintic = 2.0315
momentum_rate = 0.95
muon_rate = 0.05
muon_step = 0.05
decay_rate = 0.1
adam_rate = 0.5
beta_first = 0.9
beta_second = 0.95

half = jnp.bfloat16
single = jnp.float32


OUT, QKV, HID, DOWN = 0, 1, 2, 3
ROWS = (D, 3 * D, FF, FF)


def norm_rows(values, gain, shift):
    center = values - jnp.mean(values, axis=-1, keepdims=True)
    spread = jnp.mean(center * center, axis=-1, keepdims=True)
    return center * lax.rsqrt(spread + 1e-05) * gain + shift


def gelu_tanh(values):
    return jax.nn.gelu(values, approximate=True)


def split_small(packed):
    pieces = []
    offset = 0
    for width in (D, D, D, FF, D, D, D, D, D):
        pieces.append(packed[offset : offset + width])
        offset = offset + width
    return pieces


def contract_rows(left, right):
    return lax.dot_general(
        left, right, (((0,), (0,)), ((), ())), preferred_element_type=jnp.float32
    )


def dot_nt(left, right):
    return lax.dot_general(
        left, right, (((1,), (1,)), ((), ())), preferred_element_type=jnp.float32
    )


def dot_nn(left, right):
    return jnp.dot(left, right, preferred_element_type=jnp.float32)


QB = 256


def scores_t(query, keys, seg_col, seg_row, start):
    count, width = keys.shape[0], query.shape[0]
    scores = dot_nt(keys, query) * 0.125
    key_pos = lax.broadcasted_iota(jnp.int32, (count, width), 0)
    query_pos = start + lax.broadcasted_iota(jnp.int32, (count, width), 1)
    allowed = (key_pos <= query_pos) & (seg_col[:count] == seg_row[:, start : start + width])
    return jnp.where(allowed, scores, -1e30)


def attend_kernel(q_ref, k_ref, v_ref, col_ref, row_ref, out_ref):
    length = q_ref.shape[0]
    seg_col = col_ref[...]
    seg_row = row_ref[...]
    for head in range(2):
        lanes = slice(head * HD, (head + 1) * HD)
        query, keys = q_ref[:, lanes], k_ref[:, lanes]
        value_t = v_ref[:, lanes].T
        for start in range(0, length, QB):
            stop = start + QB
            masked = scores_t(query[start:stop], keys[:stop], seg_col, seg_row, start)
            top = jnp.max(masked, axis=0, keepdims=True)
            weights = jnp.exp(masked - top)
            total = jnp.sum(weights, axis=0, keepdims=True)
            mixed = dot_nn(value_t[:, :stop], weights.astype(half)) / total
            out_ref[start:stop, lanes] = mixed.T.astype(half)


def attend_back_kernel(q_ref, k_ref, v_ref, g_ref, col_ref, row_ref, out_ref, key_acc, value_acc):
    length = q_ref.shape[0]
    seg_col = col_ref[...]
    seg_row = row_ref[...]
    for head in range(2):
        lanes = slice(head * HD, (head + 1) * HD)
        query, keys, values = q_ref[:, lanes], k_ref[:, lanes], v_ref[:, lanes]
        grads = g_ref[:, lanes]
        key_t = keys.T
        key_acc[...] = jnp.zeros_like(key_acc)
        value_acc[...] = jnp.zeros_like(value_acc)
        for start in range(0, length, QB):
            stop = start + QB
            masked = scores_t(query[start:stop], keys[:stop], seg_col, seg_row, start)
            top = jnp.max(masked, axis=0, keepdims=True)
            weights = jnp.exp(masked - top)
            prob = weights / jnp.sum(weights, axis=0, keepdims=True)
            prob_grad = dot_nt(values[:stop], grads[start:stop])
            delta = jnp.sum(prob * prob_grad, axis=0, keepdims=True)
            score_grad = (prob * (prob_grad - delta)).astype(half)
            value_acc[:stop] += dot_nn(prob.astype(half), grads[start:stop])
            key_acc[:stop] += dot_nn(score_grad, query[start:stop])
            query_grad = dot_nn(key_t[:, :stop], score_grad) * 0.125
            out_ref[0, start:stop, lanes] = query_grad.T.astype(half)
        out_ref[1, :, lanes] = (key_acc[...] * 0.125).astype(half)
        out_ref[2, :, lanes] = value_acc[...].astype(half)


def attend(heads_qkv, seg_col, seg_row):
    length = heads_qkv.shape[0]
    width = heads_qkv.shape[1] // 3
    pairs = width // (2 * HD)
    lane_spec = lambda part: pl.BlockSpec((length, 2 * HD), lambda h: (0, part * pairs + h))
    return pl.pallas_call(
        attend_kernel,
        grid=(pairs,),
        in_specs=[
            lane_spec(0),
            lane_spec(1),
            lane_spec(2),
            pl.BlockSpec((length, 1), lambda h: (0, 0)),
            pl.BlockSpec((1, length), lambda h: (0, 0)),
        ],
        out_specs=pl.BlockSpec((length, 2 * HD), lambda h: (0, h)),
        out_shape=jax.ShapeDtypeStruct((length, width), half),
        name="attend",
    )(heads_qkv, heads_qkv, heads_qkv, seg_col, seg_row)


def attend_back(heads_qkv, grads, seg_col, seg_row):
    length = heads_qkv.shape[0]
    width = heads_qkv.shape[1] // 3
    pairs = width // (2 * HD)
    lane_spec = lambda part: pl.BlockSpec((length, 2 * HD), lambda h: (0, part * pairs + h))
    return pl.pallas_call(
        attend_back_kernel,
        grid=(pairs,),
        in_specs=[
            lane_spec(0),
            lane_spec(1),
            lane_spec(2),
            lane_spec(0),
            pl.BlockSpec((length, 1), lambda h: (0, 0)),
            pl.BlockSpec((1, length), lambda h: (0, 0)),
        ],
        out_specs=pl.BlockSpec((3, length, 2 * HD), lambda h: (0, 0, h)),
        out_shape=jax.ShapeDtypeStruct((3, length, width), half),
        scratch_shapes=[pltpu.VMEM((length, HD), single), pltpu.VMEM((length, HD), single)],
        name="attend_back",
    )(heads_qkv, heads_qkv, heads_qkv, grads, seg_col, seg_row)


NB = 256


def newton_kernel(
    gram_ref, x_ref, out_ref, gram, gram_h, gram_l, poly_h, poly_l, prod_h, prod_l, y_h, y_l
):
    size = gram_ref.shape[0]
    count = x_ref.shape[0]

    def block(index):
        return pl.ds(pl.multiple_of(index * NB, NB), NB)

    def over(total, step):
        def go(index, carry):
            step(block(index), index)
            return carry

        lax.fori_loop(0, total // NB, go, 0)

    def store(high, low, rows, value):
        top = value.astype(half)
        high[rows] = top
        low[rows] = (value - top.astype(single)).astype(half)

    def product(left_h, left_l, right_h, right_l, rows):
        lead = left_h[rows]
        tail = left_l[rows]
        whole = right_h[...]
        return dot_nn(lead, whole) + (dot_nn(lead, right_l[...]) + dot_nn(tail, whole))

    def eye(index):
        row = lax.broadcasted_iota(jnp.int32, (NB, size), 0) + index * NB
        col = lax.broadcasted_iota(jnp.int32, (NB, size), 1)
        return row == col

    def trace_step(index, total):
        return total + jnp.sum(jnp.where(eye(index), gram_ref[block(index)], 0.0))

    trace = lax.fori_loop(0, size // NB, trace_step, jnp.float32(0.0))
    scale = jnp.full((1, 1), jnp.sqrt(jnp.full((1, 1), trace, single)) + 1e-07)
    square = scale * scale

    def load_gram(rows, index):
        value = gram_ref[rows] / square
        gram[rows] = value
        store(gram_h, gram_l, rows, value)

    over(size, load_gram)

    def load_x(rows, index):
        store(y_h, y_l, rows, x_ref[rows] / scale)

    over(count, load_x)

    def sweep(_, carry):
        def poly(rows, index):
            twice = product(gram_h, gram_l, gram_h, gram_l, rows)
            value = poly_cubic * gram[rows] + poly_quintic * twice
            value = value + jnp.where(eye(index), poly_linear, 0.0)
            store(poly_h, poly_l, rows, value)

        over(size, poly)

        def middle(rows, index):
            store(prod_h, prod_l, rows, product(poly_h, poly_l, gram_h, gram_l, rows))

        over(size, middle)

        def apply(rows, index):
            store(y_h, y_l, rows, product(y_h, y_l, poly_h, poly_l, rows))

        over(count, apply)

        def outer(rows, index):
            value = product(prod_h, prod_l, poly_h, poly_l, rows)
            gram[rows] = value

        over(size, outer)

        def resplit(rows, index):
            store(gram_h, gram_l, rows, gram[rows])

        over(size, resplit)
        return carry

    lax.fori_loop(0, ITERS - 1, sweep, 0)

    def last(rows, index):
        once = product(y_h, y_l, gram_h, gram_l, rows)
        store(prod_h, prod_l, rows, once)
        twice = product(prod_h, prod_l, gram_h, gram_l, rows)
        own = y_h[rows].astype(single) + y_l[rows].astype(single)
        value = poly_linear * own + poly_cubic * once + poly_quintic * twice
        out_ref[rows] = value.astype(half)

    over(count, last)


def newton(gram, rows):
    size, count = gram.shape[0], rows.shape[0]
    square = lambda kind: pltpu.VMEM((size, size), kind)
    return pl.pallas_call(
        newton_kernel,
        in_specs=[pl.BlockSpec(memory_space=pltpu.VMEM)] * 2,
        out_specs=pl.BlockSpec(memory_space=pltpu.VMEM),
        out_shape=jax.ShapeDtypeStruct((count, size), half),
        scratch_shapes=[square(single)]
        + [square(half)] * 6
        + [pltpu.VMEM((count, size), half)] * 2,
        name="newton",
    )(gram, rows)


class Net:
    def __init__(self):
        self.dp = lax.axis_size("dp")
        self.ctx = lax.axis_size("ctx")
        self.d = lax.axis_index("dp")
        self.c = lax.axis_index("ctx")
        self.core = self.d & 1
        self.site = self.d >> 1
        self.levels = (self.dp // 2).bit_length() - 1
        self.plane_of = [index * (self.ctx // 4) for index in range(4)]
        self.piece = FF // (self.dp * self.ctx)
        self.chunk = FF // self.dp
        self.own = [rows // (self.dp * self.ctx) for rows in ROWS]

    def mask(self, core, step):
        shift = step if core == 0 else (step + self.levels // 2) % self.levels
        return 1 << shift

    def step_mask(self, step):
        return jnp.where(self.core == 0, self.mask(0, step), self.mask(1, step))

    def swap_core(self, value):
        return lax.ppermute(value, "dp", [(i, i ^ 1) for i in range(self.dp)])

    def swap_site(self, value, step):
        pairs = [(i, i ^ (self.mask(i & 1, step) << 1)) for i in range(self.dp)]
        return lax.ppermute(value, "dp", pairs)

    def relative(self, t):
        out = jnp.int32(0)
        for step in range(self.levels):
            if (t >> step) & 1:
                out = out ^ self.step_mask(step)
        return out

    def at(self, table):
        return jnp.take(jnp.array(table, jnp.int32), self.c)

    def reduce_sites(self, parts):
        count, rows, width = parts.shape
        split = parts.reshape(count // 2, 2, rows, width)
        pick = lambda which: lax.dynamic_index_in_dim(split, which, 1, keepdims=False)
        mine = pick(self.core)
        other = self.swap_core(pick(1 - self.core))
        total = (mine.astype(single) + other.astype(single)).astype(half)
        alive = range(1 << self.levels)
        held = {
            t: lax.dynamic_index_in_dim(total, self.site ^ self.relative(t), 0, keepdims=False)
            for t in alive
        }
        for step in range(self.levels):
            leave = [t for t in alive if (t >> step) & 1]
            came = self.swap_site(jnp.concatenate([held[t] for t in leave], 0), step)
            for slot, t in enumerate(leave):
                stay = t ^ (1 << step)
                piece = came[slot * rows : (slot + 1) * rows]
                held[stay] = (held[stay].astype(single) + piece.astype(single)).astype(half)
            alive = [t for t in alive if not (t >> step) & 1]
        return held[0]

    def reduce_planes(self, stack, offsets, rows):
        table = [offsets.get(plane, 0) for plane in range(self.ctx)]
        take = lambda plane: lax.dynamic_slice_in_dim(
            stack, jnp.take(jnp.array(table, jnp.int32), plane), rows, 0
        )
        total = take(self.c).astype(single)
        for shift in range(1, self.ctx):
            pairs = [((plane + shift) % self.ctx, plane) for plane in offsets]
            payload = take((self.c - shift) % self.ctx)
            total = total + lax.ppermute(payload, "ctx", pairs).astype(single)
        return total

    def gather_plane(self, pieces):
        pad = lambda value: jnp.pad(value, ((0, self.piece - value.shape[0]), (0, 0)))
        which = [0] * self.ctx
        for index, plane in enumerate(self.plane_of):
            which[plane] = index
        stack = jnp.stack([pad(value) for value in pieces])
        table = jnp.array(which, jnp.int32)
        take = lambda plane: lax.dynamic_index_in_dim(
            stack, jnp.take(table, plane), 0, keepdims=False
        )
        came = [take(self.c)]
        for shift in range(1, self.ctx):
            pairs = [((plane - shift) % self.ctx, plane) for plane in self.plane_of]
            payload = take((self.c + shift) % self.ctx)
            came.append(lax.ppermute(payload, "ctx", pairs))
        came = jnp.stack(came)
        step = self.at([self.own[which[plane]] for plane in range(self.ctx)])
        out = jnp.zeros((self.chunk + self.piece, D), came.dtype)
        for source in range(self.ctx):
            part = lax.dynamic_index_in_dim(came, (self.c - source) % self.ctx, 0, keepdims=False)
            out = lax.dynamic_update_slice_in_dim(out, part, source * step, 0)
        return out[: self.chunk]

    def scatter_plane(self, rows):
        which = [0] * self.ctx
        for index, plane in enumerate(self.plane_of):
            which[plane] = index
        step = self.at([self.own[which[plane]] for plane in range(self.ctx)])
        padded = jnp.pad(rows, ((0, self.piece), (0, 0)))
        take = lambda owner: lax.dynamic_slice_in_dim(padded, owner * step, self.piece, 0)
        came = [take(self.c)]
        for shift in range(1, self.ctx):
            pairs = [(plane, (plane + shift) % self.ctx) for plane in self.plane_of]
            payload = take((self.c + shift) % self.ctx)
            came.append(lax.ppermute(payload, "ctx", pairs))
        came = jnp.stack(came)
        return [
            lax.dynamic_index_in_dim(
                came, (self.c - self.plane_of[index]) % self.ctx, 0, keepdims=False
            )[: self.own[index]]
            for index in range(4)
        ]

    def sum_gram(self, gram):
        split = gram.reshape(2, D // 2, D)
        pick = lambda which: lax.dynamic_index_in_dim(split, which, 0, keepdims=False)
        total = pick(self.core) + self.swap_core(pick(1 - self.core))
        for step in range(self.levels):
            total = total + self.swap_site(total, step)
        other = self.swap_core(total)
        first = jnp.where(self.core == 0, total, other)
        second = jnp.where(self.core == 0, other, total)
        return jnp.concatenate([first, second], 0)


def to_heads(net, value):
    positions, parts, _ = value.shape
    width = D // net.ctx
    split = value.reshape(positions, parts, net.ctx, width)
    sent = jnp.transpose(split, (2, 0, 1, 3)).reshape(net.ctx, positions, parts * width)
    came = lax.all_to_all(sent, "ctx", 0, 0, tiled=True)
    return came.reshape(net.ctx * positions, parts * width)


def from_heads(net, value):
    parts, length, width = value.shape
    positions = length // net.ctx
    sent = jnp.transpose(value.reshape(parts, net.ctx, positions, width), (1, 2, 0, 3))
    came = lax.all_to_all(sent, "ctx", 0, 0, tiled=True)
    return jnp.transpose(came, (1, 2, 0, 3)).reshape(positions, parts * D)


def body(
    tokens,
    cotangent,
    segments,
    qkv_weight,
    output_weight,
    hidden_weight,
    down_weight,
    small_params,
    qkv_moment,
    output_moment,
    hidden_moment,
    down_moment,
    adam_first,
    adam_second,
):
    net = Net()
    both = ("dp", "ctx")
    gather = lambda value: lax.all_gather(value.astype(half), both, axis=0, tiled=True)
    qkv_w = gather(qkv_weight.T)
    small_low = gather(small_params)
    output_w = gather(output_weight.T)
    hidden_w = gather(hidden_weight.T)
    down_w = gather(down_weight)
    moment_rows = net.gather_plane([output_moment.T, qkv_moment.T, hidden_moment.T, down_moment])
    (
        query_bias,
        value_bias,
        output_bias,
        hidden_bias,
        down_bias,
        attn_gain,
        attn_shift,
        mlp_gain,
        mlp_shift,
    ) = [piece.astype(single) for piece in split_small(small_low)]
    local_pos = tokens.shape[0]
    rows = tokens.astype(single).reshape(local_pos, D)
    seg_row = segments
    seg_col = segments.reshape(-1, 1)

    norm_one, pull_one = jax.vjp(norm_rows, rows, attn_gain, attn_shift)
    normed_one = norm_one.astype(half)
    bias = jnp.concatenate([query_bias, jnp.zeros((D,), single), value_bias])
    qkv = (dot_nt(normed_one, qkv_w) + bias).astype(half)
    heads_qkv = to_heads(net, qkv.reshape(local_pos, 3, D))
    mix_heads = attend(heads_qkv, seg_col, seg_row)
    mix_low = from_heads(net, mix_heads[None])
    middle = rows + dot_nt(mix_low, output_w) + output_bias
    norm_two, pull_two = jax.vjp(norm_rows, middle, mlp_gain, mlp_shift)
    normed_two = norm_two.astype(half)
    hidden_pre = dot_nt(normed_two, hidden_w) + hidden_bias
    activated, pull_act = jax.vjp(gelu_tanh, hidden_pre)
    act_low = activated.astype(half)
    result = middle + dot_nn(act_low, down_w) + down_bias
    block_out = result.astype(half).reshape(tokens.shape)

    pull_low = cotangent.reshape(local_pos, D)
    down_grad = contract_rows(act_low, pull_low).astype(half)
    down_bias_grad = pull_low.astype(single).sum(0)
    act_grad = dot_nt(pull_low, down_w)
    pre_grad = pull_act(act_grad)[0].astype(half)
    hidden_grad = contract_rows(pre_grad, normed_two).astype(half)
    hidden_bias_grad = pre_grad.astype(single).sum(0)
    normed_grad = dot_nn(pre_grad, hidden_w)
    middle_part, mlp_gain_grad, mlp_shift_grad = pull_two(normed_grad)
    mid_grad = pull_low.astype(single) + middle_part
    branch_grad = mid_grad.astype(half)
    output_grad = contract_rows(branch_grad, mix_low).astype(half)
    output_bias_grad = branch_grad.astype(single).sum(0)
    mix_grad = dot_nn(branch_grad, output_w).astype(half)

    by_dp = lambda value: value.reshape(net.dp, -1, D)
    early = net.reduce_sites(
        jnp.concatenate([by_dp(hidden_grad), by_dp(down_grad), by_dp(output_grad)], 1)
    )
    early = jnp.pad(early, ((0, net.chunk - D // net.dp), (0, 0)))

    grad_heads = to_heads(net, mix_grad.reshape(local_pos, 1, D))
    qkv_rows = from_heads(net, attend_back(heads_qkv, grad_heads, seg_col, seg_row))
    qkv_grad = contract_rows(qkv_rows, normed_one).astype(half)
    column_sums = qkv_rows.astype(single).sum(0)
    normed_one_grad = dot_nn(qkv_rows, qkv_w)
    input_part, attn_gain_grad, attn_shift_grad = pull_one(normed_one_grad)
    input_grad = (mid_grad + input_part).reshape(tokens.shape)

    planes = net.plane_of
    early_rows = net.reduce_planes(
        early,
        {planes[HID]: 0, planes[DOWN]: net.chunk, planes[OUT]: 2 * net.chunk},
        net.chunk,
    )
    late = net.reduce_sites(by_dp(qkv_grad))
    late_rows = net.reduce_planes(late, {planes[QKV]: 0}, late.shape[0])
    late_rows = jnp.pad(late_rows, ((0, net.chunk - late.shape[0]), (0, 0)))
    grad_rows = jnp.where(net.c == planes[QKV], late_rows, early_rows)

    x_rows = momentum_rate * moment_rows + grad_rows
    gram = lax.dot_general(
        x_rows,
        x_rows,
        (((0,), (0,)), ((), ())),
        precision=lax.Precision.HIGHEST,
        preferred_element_type=single,
    )
    ortho_rows = newton(net.sum_gram(gram), x_rows)

    small_grad = jnp.concatenate(
        [
            column_sums[:D],
            column_sums[2 * D :],
            output_bias_grad,
            hidden_bias_grad,
            down_bias_grad,
            attn_gain_grad,
            attn_shift_grad,
            mlp_gain_grad,
            mlp_shift_grad,
        ]
    )
    small_sum = lax.psum_scatter(small_grad, both, scatter_dimension=0, tiled=True)

    sums = [value.astype(single) for value in net.scatter_plane(grad_rows.astype(half))]
    orthos = [value.astype(single) for value in net.scatter_plane(ortho_rows)]
    natural = lambda values: (values[QKV].T, values[OUT].T, values[HID].T, values[DOWN])
    sums = natural(sums)
    orthos = natural(orthos)
    old_moments = (qkv_moment, output_moment, hidden_moment, down_moment)
    moments = [momentum_rate * old_moments[index] + sums[index] for index in range(4)]
    largest = (3 * D, D, max(D, FF), max(D, FF))
    weights_now = (qkv_weight, output_weight, hidden_weight, down_weight)
    updated = [
        weights_now[index] * (1.0 - muon_rate * decay_rate)
        - muon_step * math.sqrt(largest[index]) * orthos[index]
        for index in range(4)
    ]
    new_first = beta_first * adam_first + (1.0 - beta_first) * small_sum
    new_second = beta_second * adam_second + (1.0 - beta_second) * small_sum * small_sum
    corrected = (
        new_first
        / (1.0 - beta_first**STEP)
        / (jnp.sqrt(new_second / (1.0 - beta_second**STEP)) + 1e-08)
    )
    new_small = small_params - adam_rate * corrected
    return (
        block_out,
        input_grad,
        sums[0],
        sums[1],
        sums[2],
        sums[3],
        small_sum,
        updated[0],
        updated[1],
        updated[2],
        updated[3],
        new_small,
        moments[0],
        moments[1],
        moments[2],
        moments[3],
        new_first,
        new_second,
    )


def solution(mesh):
    in_specs = (
        P("ctx", "dp", None),
        P("ctx", "dp", None),
        P("dp", None),
        P(None, ("dp", "ctx")),
        P(None, ("dp", "ctx")),
        P(None, ("dp", "ctx")),
        P(("dp", "ctx"), None),
        P(("dp", "ctx")),
        P(None, ("dp", "ctx")),
        P(None, ("dp", "ctx")),
        P(None, ("dp", "ctx")),
        P(("dp", "ctx"), None),
        P(("dp", "ctx")),
        P(("dp", "ctx")),
    )
    out_specs = (
        P("ctx", "dp", None),
        P("ctx", "dp", None),
        P(None, ("dp", "ctx")),
        P(None, ("dp", "ctx")),
        P(None, ("dp", "ctx")),
        P(("dp", "ctx"), None),
        P(("dp", "ctx")),
        P(None, ("dp", "ctx")),
        P(None, ("dp", "ctx")),
        P(None, ("dp", "ctx")),
        P(("dp", "ctx"), None),
        P(("dp", "ctx")),
        P(None, ("dp", "ctx")),
        P(None, ("dp", "ctx")),
        P(None, ("dp", "ctx")),
        P(("dp", "ctx"), None),
        P(("dp", "ctx")),
        P(("dp", "ctx")),
    )
    return jax.shard_map(body, mesh=mesh, in_specs=in_specs, out_specs=out_specs, check_vma=False)
```

```python
import math

import jax
import jax.numpy as jnp
from jax import lax
from jax.experimental import pallas as pl
from jax.experimental.pallas import tpu as pltpu
from jax.sharding import PartitionSpec as P

D = 1024
H = 16
HD = 64
FF = 4096
ITERS = 5
STEP = 4

poly_linear = 3.4445
poly_cubic = -4.775
poly_quintic = 2.0315
momentum_rate = 0.95
muon_rate = 0.05
muon_step = 0.05
decay_rate = 0.1
adam_rate = 0.5
beta_first = 0.9
beta_second = 0.95

half = jnp.bfloat16
single = jnp.float32


OUT, QKV, HID, DOWN = 0, 1, 2, 3
ROWS = (D, 3 * D, FF, FF)


def norm_rows(values, gain, shift):
    center = values - jnp.mean(values, axis=-1, keepdims=True)
    spread = jnp.mean(center * center, axis=-1, keepdims=True)
    return center * lax.rsqrt(spread + 1e-05) * gain + shift


def gelu_tanh(values):
    return jax.nn.gelu(values, approximate=True)


def split_small(packed):
    pieces = []
    offset = 0
    for width in (D, D, D, FF, D, D, D, D, D):
        pieces.append(packed[offset : offset + width])
        offset = offset + width
    return pieces


def contract_rows(left, right):
    return lax.dot_general(
        left, right, (((0,), (0,)), ((), ())), preferred_element_type=jnp.float32
    )


def dot_nt(left, right):
    return lax.dot_general(
        left, right, (((1,), (1,)), ((), ())), preferred_element_type=jnp.float32
    )


def dot_nn(left, right):
    return jnp.dot(left, right, preferred_element_type=jnp.float32)


QB = 256


def scores_t(query, keys, seg_col, seg_row, start):
    count, width = keys.shape[0], query.shape[0]
    scores = dot_nt(keys, query) * 0.125
    key_pos = lax.broadcasted_iota(jnp.int32, (count, width), 0)
    query_pos = start + lax.broadcasted_iota(jnp.int32, (count, width), 1)
    allowed = (key_pos <= query_pos) & (seg_col[:count] == seg_row[:, start : start + width])
    return jnp.where(allowed, scores, -1e30)


def attend_kernel(q_ref, k_ref, v_ref, col_ref, row_ref, out_ref):
    length = q_ref.shape[0]
    seg_col = col_ref[...]
    seg_row = row_ref[...]
    for head in range(2):
        lanes = slice(head * HD, (head + 1) * HD)
        query, keys = q_ref[:, lanes], k_ref[:, lanes]
        value_t = v_ref[:, lanes].T
        for start in range(0, length, QB):
            stop = start + QB
            masked = scores_t(query[start:stop], keys[:stop], seg_col, seg_row, start)
            top = jnp.max(masked, axis=0, keepdims=True)
            weights = jnp.exp(masked - top)
            total = jnp.sum(weights, axis=0, keepdims=True)
            mixed = dot_nn(value_t[:, :stop], weights.astype(half)) / total
            out_ref[start:stop, lanes] = mixed.T.astype(half)


def attend_back_kernel(q_ref, k_ref, v_ref, g_ref, col_ref, row_ref, out_ref, key_acc, value_acc):
    length = q_ref.shape[0]
    seg_col = col_ref[...]
    seg_row = row_ref[...]
    for head in range(2):
        lanes = slice(head * HD, (head + 1) * HD)
        query, keys, values = q_ref[:, lanes], k_ref[:, lanes], v_ref[:, lanes]
        grads = g_ref[:, lanes]
        key_t = keys.T
        key_acc[...] = jnp.zeros_like(key_acc)
        value_acc[...] = jnp.zeros_like(value_acc)
        for start in range(0, length, QB):
            stop = start + QB
            masked = scores_t(query[start:stop], keys[:stop], seg_col, seg_row, start)
            top = jnp.max(masked, axis=0, keepdims=True)
            weights = jnp.exp(masked - top)
            prob = weights / jnp.sum(weights, axis=0, keepdims=True)
            prob_grad = dot_nt(values[:stop], grads[start:stop])
            delta = jnp.sum(prob * prob_grad, axis=0, keepdims=True)
            score_grad = (prob * (prob_grad - delta)).astype(half)
            value_acc[:stop] += dot_nn(prob.astype(half), grads[start:stop])
            key_acc[:stop] += dot_nn(score_grad, query[start:stop])
            query_grad = dot_nn(key_t[:, :stop], score_grad) * 0.125
            out_ref[0, start:stop, lanes] = query_grad.T.astype(half)
        out_ref[1, :, lanes] = (key_acc[...] * 0.125).astype(half)
        out_ref[2, :, lanes] = value_acc[...].astype(half)


def attend(heads_qkv, seg_col, seg_row):
    length = heads_qkv.shape[0]
    width = heads_qkv.shape[1] // 3
    pairs = width // (2 * HD)
    lane_spec = lambda part: pl.BlockSpec((length, 2 * HD), lambda h: (0, part * pairs + h))
    return pl.pallas_call(
        attend_kernel,
        grid=(pairs,),
        in_specs=[
            lane_spec(0),
            lane_spec(1),
            lane_spec(2),
            pl.BlockSpec((length, 1), lambda h: (0, 0)),
            pl.BlockSpec((1, length), lambda h: (0, 0)),
        ],
        out_specs=pl.BlockSpec((length, 2 * HD), lambda h: (0, h)),
        out_shape=jax.ShapeDtypeStruct((length, width), half),
        name="attend",
    )(heads_qkv, heads_qkv, heads_qkv, seg_col, seg_row)


def attend_back(heads_qkv, grads, seg_col, seg_row):
    length = heads_qkv.shape[0]
    width = heads_qkv.shape[1] // 3
    pairs = width // (2 * HD)
    lane_spec = lambda part: pl.BlockSpec((length, 2 * HD), lambda h: (0, part * pairs + h))
    return pl.pallas_call(
        attend_back_kernel,
        grid=(pairs,),
        in_specs=[
            lane_spec(0),
            lane_spec(1),
            lane_spec(2),
            lane_spec(0),
            pl.BlockSpec((length, 1), lambda h: (0, 0)),
            pl.BlockSpec((1, length), lambda h: (0, 0)),
        ],
        out_specs=pl.BlockSpec((3, length, 2 * HD), lambda h: (0, 0, h)),
        out_shape=jax.ShapeDtypeStruct((3, length, width), half),
        scratch_shapes=[pltpu.VMEM((length, HD), single), pltpu.VMEM((length, HD), single)],
        name="attend_back",
    )(heads_qkv, heads_qkv, heads_qkv, grads, seg_col, seg_row)


NB = 256
PACKED = 2 * NB + NB // 2


def split_halves(value):
    top = value.astype(half)
    return top, (value - top.astype(single)).astype(half)


def gram_kernel(x_ref, out_ref, row_h, row_l, col_h, col_l):
    value = x_ref[...]
    top, tail = split_halves(value)
    row_h[...] = top
    row_l[...] = tail
    top, tail = split_halves(value.T)
    col_h[...] = top
    col_l[...] = tail
    for index in range(D // NB):
        rows = slice(index * NB, (index + 1) * NB)
        lead = col_h[rows]
        whole = row_h[:, index * NB :]
        panel = dot_nn(lead, whole) + (
            dot_nn(lead, row_l[:, index * NB :]) + dot_nn(col_l[rows], whole)
        )
        if index == 0:
            out_ref[:NB] = panel
        elif index == 1:
            out_ref[NB : 2 * NB, : 3 * NB] = panel
        elif index == 2:
            out_ref[2 * NB :, : 2 * NB] = panel[: NB // 2]
            out_ref[2 * NB :, 2 * NB :] = panel[NB // 2 :]
        else:
            out_ref[NB : 2 * NB, 3 * NB :] = panel


def packed_gram(rows):
    count = rows.shape[0]
    return pl.pallas_call(
        gram_kernel,
        in_specs=[pl.BlockSpec(memory_space=pltpu.VMEM)],
        out_specs=pl.BlockSpec(memory_space=pltpu.VMEM),
        out_shape=jax.ShapeDtypeStruct((PACKED, D), single),
        scratch_shapes=[pltpu.VMEM((count, D), half)] * 2 + [pltpu.VMEM((D, count), half)] * 2,
        name="packed_gram",
    )(rows)


def newton_kernel(
    core_ref, mine_ref, other_ref, x_ref, out_ref,
    pack, gram_h, gram_l, poly_h, poly_l, prod_h, prod_l, y_h, y_l,
):
    count = x_ref.shape[0]
    blocks = D // NB

    @pl.when(core_ref[0] == 0)
    def _():
        pack[: PACKED // 2] = mine_ref[...]
        pack[PACKED // 2 :] = other_ref[...]

    @pl.when(core_ref[0] != 0)
    def _():
        pack[: PACKED // 2] = other_ref[...]
        pack[PACKED // 2 :] = mine_ref[...]

    def panel(index):
        if index == 0:
            return pack[:NB]
        if index == 1:
            return pack[NB : 2 * NB, : 3 * NB]
        if index == 2:
            return jnp.concatenate([pack[2 * NB :, : 2 * NB], pack[2 * NB :, 2 * NB :]], 0)
        return pack[NB : 2 * NB, 3 * NB :]

    row = lax.broadcasted_iota(jnp.int32, (NB, NB), 0)
    col = lax.broadcasted_iota(jnp.int32, (NB, NB), 1)
    trace = jnp.zeros((1, 1), single)
    for index in range(blocks):
        corner = jnp.where(row == col, panel(index)[:, :NB], 0.0)
        trace = trace + jnp.sum(jnp.sum(corner, axis=1, keepdims=True), axis=0, keepdims=True)
    scale = jnp.sqrt(trace) + 1e-07
    square = scale * scale

    def store(high, low, index, value):
        rows = slice(index * NB, (index + 1) * NB)
        top, tail = split_halves(value)
        high[rows, index * NB :] = top
        low[rows, index * NB :] = tail
        for other in range(index + 1, blocks):
            down = slice(other * NB, (other + 1) * NB)
            top, tail = split_halves(value[:, (other - index) * NB : (other - index + 1) * NB].T)
            high[down, rows] = top
            low[down, rows] = tail

    def upper(left_h, left_l, right_h, right_l, index):
        rows = slice(index * NB, (index + 1) * NB)
        lead, whole = left_h[rows], right_h[:, index * NB :]
        return dot_nn(lead, whole) + (
            dot_nn(lead, right_l[:, index * NB :]) + dot_nn(left_l[rows], whole)
        )

    def full(left_h, left_l, right_h, right_l, rows):
        lead, whole = left_h[rows], right_h[...]
        return dot_nn(lead, whole) + (dot_nn(lead, right_l[...]) + dot_nn(left_l[rows], whole))

    for index in range(blocks):
        store(gram_h, gram_l, index, panel(index) / square)
    y_rows = [slice(first, first + NB) for first in range(0, count, NB)]
    for rows in y_rows:
        top, tail = split_halves(x_ref[rows] / scale)
        y_h[rows] = top
        y_l[rows] = tail

    def sweep(_, carry):
        for index in range(blocks):
            rows = slice(index * NB, (index + 1) * NB)
            own = gram_h[rows, index * NB :].astype(single) + gram_l[rows, index * NB :].astype(
                single
            )
            value = poly_cubic * own + poly_quintic * upper(gram_h, gram_l, gram_h, gram_l, index)
            width = value.shape[1]
            diagonal = lax.broadcasted_iota(jnp.int32, (NB, width), 0) == lax.broadcasted_iota(
                jnp.int32, (NB, width), 1
            )
            store(poly_h, poly_l, index, value + jnp.where(diagonal, poly_linear, 0.0))
        for index in range(blocks):
            store(prod_h, prod_l, index, upper(poly_h, poly_l, gram_h, gram_l, index))
        for index in range(blocks):
            store(gram_h, gram_l, index, upper(prod_h, prod_l, poly_h, poly_l, index))
        for rows in y_rows:
            top, tail = split_halves(full(y_h, y_l, poly_h, poly_l, rows))
            y_h[rows] = top
            y_l[rows] = tail
        return carry

    lax.fori_loop(0, ITERS - 1, sweep, 0)
    for rows in y_rows:
        once = full(y_h, y_l, gram_h, gram_l, rows)
        top, tail = split_halves(once)
        prod_h[rows] = top
        prod_l[rows] = tail
        twice = full(prod_h, prod_l, gram_h, gram_l, rows)
        own = y_h[rows].astype(single) + y_l[rows].astype(single)
        value = poly_linear * own + poly_cubic * once + poly_quintic * twice
        out_ref[rows] = value.astype(half)


def newton(core, mine, other, rows):
    count = rows.shape[0]
    return pl.pallas_call(
        newton_kernel,
        in_specs=[pl.BlockSpec(memory_space=pltpu.SMEM)]
        + [pl.BlockSpec(memory_space=pltpu.VMEM)] * 3,
        out_specs=pl.BlockSpec(memory_space=pltpu.VMEM),
        out_shape=jax.ShapeDtypeStruct((count, D), half),
        scratch_shapes=[pltpu.VMEM((PACKED, D), single)]
        + [pltpu.VMEM((D, D), half)] * 6
        + [pltpu.VMEM((count, D), half)] * 2,
        name="newton",
    )(core.reshape(1), mine, other, rows)


def after(value, *earlier):
    return lax.optimization_barrier((value,) + earlier)[0]


class Net:
    def __init__(self):
        self.dp = lax.axis_size("dp")
        self.ctx = lax.axis_size("ctx")
        self.d = lax.axis_index("dp")
        self.c = lax.axis_index("ctx")
        self.core = self.d & 1
        self.site = self.d >> 1
        self.levels = (self.dp // 2).bit_length() - 1
        self.sites = 1 << self.levels
        step = self.ctx // 4
        self.plane_of = {HID: 0, QKV: step, DOWN: 2 * step, OUT: 3 * step}
        self.matrix_on = [0] * self.ctx
        for index, plane in self.plane_of.items():
            self.matrix_on[plane] = index
        self.piece = FF // (self.dp * self.ctx)
        self.chunk = FF // self.dp
        self.own = [rows // (self.dp * self.ctx) for rows in ROWS]

    def mask(self, core, step):
        shift = step if core == 0 else (step + self.levels // 2) % self.levels
        return 1 << shift

    def swap_core(self, value):
        return lax.ppermute(value, "dp", [(i, i ^ 1) for i in range(self.dp)])

    def swap_site(self, value, step):
        pairs = [(i, i ^ (self.mask(i & 1, step) << 1)) for i in range(self.dp)]
        return lax.ppermute(value, "dp", pairs)

    def shift_ctx(self, value, shift):
        return lax.ppermute(value, "ctx", [(c, (c + shift) % self.ctx) for c in range(self.ctx)])

    def relative(self, t, core):
        offset = [0, 0]
        for which in range(2):
            for step in range(self.levels):
                if (t >> step) & 1:
                    offset[which] ^= self.mask(which, step)
        return jnp.where(core == 0, offset[0], offset[1])

    def chunk_at(self, t, mine):
        core = self.core if mine else 1 - self.core
        return (self.site ^ self.relative(t, core)) * 2 + core

    def chunk_order(self):
        return [self.chunk_at(t, mine) for mine in (True, False) for t in range(self.sites)]

    def low_step(self, t):
        return (t & -t).bit_length() - 1

    def at(self, table, index):
        return jnp.take(jnp.array(table, jnp.int32), index)

    def gather(self, shard, *earlier):
        shard = after(shard, *earlier) if earlier else shard
        came = [shard] + [self.shift_ctx(shard, shift) for shift in range(1, self.ctx)]
        whole = jnp.zeros((self.ctx,) + shard.shape, shard.dtype)
        for shift, part in enumerate(came):
            whole = lax.dynamic_update_index_in_dim(
                whole, part, (self.c - shift) % self.ctx, 0
            )
        held = {0: whole}
        for t in range(1, self.sites):
            step = self.low_step(t)
            held[t] = self.swap_site(held[t ^ (1 << step)], step)
        mine = [held[t] for t in range(self.sites)]
        return mine + [self.swap_core(value) for value in mine], came[-1]

    def reduce_sites(self, keep, send):
        came = self.swap_core(jnp.stack(send))
        add = lambda a, b: (a.astype(single) + b.astype(single)).astype(keep[0].dtype)
        held = [add(keep[t], came[t]) for t in range(self.sites)]
        for t in range(self.sites - 1, 0, -1):
            step = self.low_step(t)
            to = t ^ (1 << step)
            held[to] = add(held[to], self.swap_site(held[t], step))
        return held[0]

    def reduce_dp(self, parts):
        take = lambda index: lax.dynamic_index_in_dim(parts, index, 0, keepdims=False)
        keep = [take(self.chunk_at(t, True)) for t in range(self.sites)]
        send = [take(self.chunk_at(t, False)) for t in range(self.sites)]
        return self.reduce_sites(keep, send)

    def reduce_to_plane(self, value, matrix):
        plane = self.plane_of[matrix]
        total = value.astype(single)
        for shift in range(1, self.ctx):
            came = lax.ppermute(value, "ctx", [((plane + shift) % self.ctx, plane)])
            total = total + came.astype(single)
        return total

    def spread_ctx(self, value):
        take = lambda index: lax.dynamic_index_in_dim(value, index % self.ctx, 0, keepdims=False)
        total = take(self.c)
        for shift in range(1, self.ctx):
            total = total + self.shift_ctx(take(self.c + shift), shift)
        return total

    def gather_plane(self, pieces):
        pad = lambda value: jnp.pad(value, ((0, self.piece - value.shape[0]), (0, 0)))
        stack = jnp.stack([pad(value) for value in pieces])
        take = lambda plane: lax.dynamic_index_in_dim(
            stack, self.at(self.matrix_on, plane % self.ctx), 0, keepdims=False
        )
        came = [take(self.c)]
        for shift in range(1, self.ctx):
            pairs = [((plane - shift) % self.ctx, plane) for plane in self.plane_of.values()]
            came.append(lax.ppermute(take(self.c + shift), "ctx", pairs))
        came = jnp.stack(came)
        step = self.at([self.own[index] for index in self.matrix_on], self.c)
        out = jnp.zeros((self.chunk + self.piece, D), came.dtype)
        for source in range(self.ctx):
            part = lax.dynamic_index_in_dim(came, (self.c - source) % self.ctx, 0, keepdims=False)
            out = lax.dynamic_update_slice_in_dim(out, part, source * step, 0)
        return out[: self.chunk]

    def scatter_plane(self, rows):
        step = self.at([self.own[index] for index in self.matrix_on], self.c)
        padded = jnp.pad(rows, ((0, self.piece), (0, 0)))
        take = lambda owner: lax.dynamic_slice_in_dim(
            padded, (owner % self.ctx) * step, self.piece, 0
        )
        came = [take(self.c)]
        for shift in range(1, self.ctx):
            pairs = [(plane, (plane + shift) % self.ctx) for plane in self.plane_of.values()]
            came.append(lax.ppermute(take(self.c + shift), "ctx", pairs))
        came = jnp.stack(came)
        return [
            lax.dynamic_index_in_dim(
                came, (self.c - self.plane_of[index]) % self.ctx, 0, keepdims=False
            )[: self.own[index]]
            for index in range(4)
        ]

    def sum_gram(self, packed):
        split = packed.reshape(2, PACKED // 2, D)
        pick = lambda which: lax.dynamic_index_in_dim(split, which, 0, keepdims=False)
        total = pick(self.core) + self.swap_core(pick(1 - self.core))
        for step in range(self.levels):
            total = total + self.swap_site(total, step)
        return total, self.swap_core(total)


def to_heads(net, value):
    positions, parts, _ = value.shape
    width = D // net.ctx
    split = value.reshape(positions, parts, net.ctx, width)
    sent = jnp.transpose(split, (2, 0, 1, 3)).reshape(net.ctx, positions, parts * width)
    came = lax.all_to_all(sent, "ctx", 0, 0, tiled=True)
    return came.reshape(net.ctx * positions, parts * width)


def from_heads(net, value):
    parts, length, width = value.shape
    positions = length // net.ctx
    sent = jnp.transpose(value.reshape(parts, net.ctx, positions, width), (1, 2, 0, 3))
    came = lax.all_to_all(sent, "ctx", 0, 0, tiled=True)
    return jnp.transpose(came, (1, 2, 0, 3)).reshape(positions, parts * D)


def place(net, chunks):
    out = jnp.zeros((net.dp,) + chunks[0].shape, chunks[0].dtype)
    for value, index in zip(chunks, net.chunk_order()):
        out = lax.dynamic_update_index_in_dim(out, value, index, 0)
    return out


def body(
    tokens,
    cotangent,
    segments,
    qkv_weight,
    output_weight,
    hidden_weight,
    down_weight,
    small_params,
    qkv_moment,
    output_moment,
    hidden_moment,
    down_moment,
    adam_first,
    adam_second,
):
    net = Net()
    local_pos = tokens.shape[0]
    small_count = small_params.shape[0]
    small_rows = 8
    small_shard = jnp.pad(small_params.astype(half).reshape(1, -1), ((0, small_rows - 1), (0, D - small_count)))
    first_shard = jnp.concatenate([qkv_weight.T.astype(half), small_shard], 0)
    second_shard = jnp.concatenate([output_weight.T.astype(half), hidden_weight.T.astype(half)], 0)
    first, mark = net.gather(first_shard)
    second, mark = net.gather(second_shard, mark)
    third, mark = net.gather(down_weight.astype(half), mark)
    own_qkv, own_out = net.own[QKV], net.own[OUT]
    qkv_w = place(net, [value[:, :own_qkv] for value in first]).reshape(3 * D, D)
    small_low = place(net, [value[:, own_qkv, :small_count] for value in first]).reshape(-1)
    output_w = place(net, [value[:, :own_out] for value in second]).reshape(D, D)
    hidden_w = jnp.concatenate([value[:, own_out:].reshape(-1, D) for value in second], 0)
    down_w = jnp.concatenate([value.reshape(-1, D) for value in third], 0)
    (
        query_bias,
        value_bias,
        output_bias,
        hidden_bias,
        down_bias,
        attn_gain,
        attn_shift,
        mlp_gain,
        mlp_shift,
    ) = [piece.astype(single) for piece in split_small(small_low)]
    by_chunk = hidden_bias.reshape(net.dp, -1)
    hidden_bias = jnp.concatenate(
        [lax.dynamic_index_in_dim(by_chunk, index, 0, keepdims=False) for index in net.chunk_order()]
    )
    rows = tokens.astype(single).reshape(local_pos, D)
    seg_row = segments
    seg_col = segments.reshape(-1, 1)

    norm_one, pull_one = jax.vjp(norm_rows, rows, attn_gain, attn_shift)
    normed_one = norm_one.astype(half)
    bias = jnp.concatenate([query_bias, jnp.zeros((D,), single), value_bias])
    qkv = (dot_nt(normed_one, qkv_w) + bias).astype(half)
    heads_qkv = to_heads(net, qkv.reshape(local_pos, 3, D))
    mix_heads = attend(heads_qkv, seg_col, seg_row)
    mix_low = from_heads(net, mix_heads[None])
    own_moments = {
        OUT: output_moment.T, QKV: qkv_moment.T, HID: hidden_moment.T, DOWN: down_moment
    }
    moment_rows = net.gather_plane(
        [after(own_moments[OUT], mix_low)] + [own_moments[index] for index in (QKV, HID, DOWN)]
    )
    middle = rows + dot_nt(mix_low, output_w) + output_bias
    norm_two, pull_two = jax.vjp(norm_rows, middle, mlp_gain, mlp_shift)
    normed_two = norm_two.astype(half)
    hidden_pre = dot_nt(normed_two, hidden_w) + hidden_bias
    activated, pull_act = jax.vjp(gelu_tanh, hidden_pre)
    act_low = activated.astype(half)
    result = middle + dot_nn(act_low, down_w) + down_bias
    block_out = result.astype(half).reshape(tokens.shape)

    near = FF // 2

    def reduce_units(left, right):
        part = lambda value: contract_rows(value, right).astype(half)
        send = part(left[:, near:]).reshape(net.sites, -1, D)
        keep = part(left[:, :near]).reshape(net.sites, -1, D)
        return net.reduce_sites(
            [keep[t] for t in range(net.sites)], [send[t] for t in range(net.sites)]
        )

    pull_low = cotangent.reshape(local_pos, D)
    down_total = reduce_units(act_low, pull_low)
    down_rows = net.reduce_to_plane(down_total, DOWN)
    down_bias_grad = pull_low.astype(single).sum(0)
    act_grad = dot_nt(pull_low, down_w)
    pre_grad = pull_act(act_grad)[0].astype(half)
    hidden_total = reduce_units(pre_grad, normed_two)
    hidden_rows = net.reduce_to_plane(hidden_total, HID)
    units_grad = pre_grad.astype(single).sum(0).reshape(net.dp, -1)
    hidden_bias_grad = place(net, [units_grad[index] for index in range(net.dp)]).reshape(-1)
    normed_grad = dot_nn(pre_grad, hidden_w)
    middle_part, mlp_gain_grad, mlp_shift_grad = pull_two(normed_grad)
    mid_grad = pull_low.astype(single) + middle_part
    branch_grad = mid_grad.astype(half)
    output_bias_grad = branch_grad.astype(single).sum(0)
    mix_grad = dot_nn(branch_grad, output_w).astype(half)
    grad_heads = to_heads(net, mix_grad.reshape(local_pos, 1, D))
    output_grad = contract_rows(branch_grad, mix_low).astype(half)
    output_total = net.reduce_dp(output_grad.reshape(net.dp, -1, D))
    output_rows = net.reduce_to_plane(output_total, OUT)

    qkv_rows = from_heads(net, attend_back(heads_qkv, grad_heads, seg_col, seg_row))
    qkv_grad = contract_rows(qkv_rows, normed_one).astype(half)
    qkv_total = net.reduce_dp(qkv_grad.reshape(net.dp, -1, D))
    late_rows = net.reduce_to_plane(qkv_total, QKV)
    column_sums = qkv_rows.astype(single).sum(0)
    normed_one_grad = dot_nn(qkv_rows, qkv_w)
    input_part, attn_gain_grad, attn_shift_grad = pull_one(normed_one_grad)
    input_grad = (mid_grad + input_part).reshape(tokens.shape)

    fill = lambda value: jnp.pad(value, ((0, net.chunk - value.shape[0]), (0, 0)))
    on = lambda index: net.c == net.plane_of[index]
    grad_rows = jnp.where(
        on(QKV),
        fill(late_rows),
        jnp.where(on(DOWN), down_rows, jnp.where(on(HID), hidden_rows, fill(output_rows))),
    )
    x_rows = momentum_rate * moment_rows + grad_rows
    mine, other = net.sum_gram(packed_gram(x_rows))
    ortho_rows = newton(net.core, mine, other, x_rows)

    small_grad = jnp.concatenate(
        [
            column_sums[:D],
            column_sums[2 * D :],
            output_bias_grad,
            hidden_bias_grad,
            down_bias_grad,
            attn_gain_grad,
            attn_shift_grad,
            mlp_gain_grad,
            mlp_shift_grad,
        ]
    )
    small_part = net.reduce_dp(small_grad.reshape(net.dp, net.ctx, 1, small_count))
    small_sum = net.spread_ctx(small_part).reshape(-1)

    sums = [value.astype(single) for value in net.scatter_plane(grad_rows.astype(half))]
    orthos = [value.astype(single) for value in net.scatter_plane(ortho_rows)]
    natural = lambda values: (values[QKV].T, values[OUT].T, values[HID].T, values[DOWN])
    sums = natural(sums)
    orthos = natural(orthos)
    old_moments = (qkv_moment, output_moment, hidden_moment, down_moment)
    moments = [momentum_rate * old_moments[index] + sums[index] for index in range(4)]
    largest = (3 * D, D, max(D, FF), max(D, FF))
    weights_now = (qkv_weight, output_weight, hidden_weight, down_weight)
    updated = [
        weights_now[index] * (1.0 - muon_rate * decay_rate)
        - muon_step * math.sqrt(largest[index]) * orthos[index]
        for index in range(4)
    ]
    new_first = beta_first * adam_first + (1.0 - beta_first) * small_sum
    new_second = beta_second * adam_second + (1.0 - beta_second) * small_sum * small_sum
    corrected = (
        new_first
        / (1.0 - beta_first**STEP)
        / (jnp.sqrt(new_second / (1.0 - beta_second**STEP)) + 1e-08)
    )
    new_small = small_params - adam_rate * corrected
    return (
        block_out,
        input_grad,
        sums[0],
        sums[1],
        sums[2],
        sums[3],
        small_sum,
        updated[0],
        updated[1],
        updated[2],
        updated[3],
        new_small,
        moments[0],
        moments[1],
        moments[2],
        moments[3],
        new_first,
        new_second,
    )


def solution(mesh):
    in_specs = (
        P("ctx", "dp", None),
        P("ctx", "dp", None),
        P("dp", None),
        P(None, ("dp", "ctx")),
        P(None, ("dp", "ctx")),
        P(None, ("dp", "ctx")),
        P(("dp", "ctx"), None),
        P(("dp", "ctx")),
        P(None, ("dp", "ctx")),
        P(None, ("dp", "ctx")),
        P(None, ("dp", "ctx")),
        P(("dp", "ctx"), None),
        P(("dp", "ctx")),
        P(("dp", "ctx")),
    )
    out_specs = (
        P("ctx", "dp", None),
        P("ctx", "dp", None),
        P(None, ("dp", "ctx")),
        P(None, ("dp", "ctx")),
        P(None, ("dp", "ctx")),
        P(("dp", "ctx"), None),
        P(("dp", "ctx")),
        P(None, ("dp", "ctx")),
        P(None, ("dp", "ctx")),
        P(None, ("dp", "ctx")),
        P(("dp", "ctx"), None),
        P(("dp", "ctx")),
        P(None, ("dp", "ctx")),
        P(None, ("dp", "ctx")),
        P(None, ("dp", "ctx")),
        P(("dp", "ctx"), None),
        P(("dp", "ctx")),
        P(("dp", "ctx")),
    )
    return jax.shard_map(body, mesh=mesh, in_specs=in_specs, out_specs=out_specs, check_vma=False)
```
